32 devices in a mesh: samp: 8 (over y, x, core), cent: 4 (over z).
Axes of the slice: x: 2, y: 2, z: 4, core: 2. Of those that a mesh axis runs over, the one named last changes fastest.
Arguments:
- embeddings: float32 [16384, 1024], P(('samp', 'cent')), may hold values from -40 to 40
- assignment: int32 [16384], P(('samp', 'cent')), may hold values from 0 to 2047, as said below
- owner_map: int32 [2048], replicated, may hold values from 0 to 31, as said below
Outputs:
- centroid: float32 [2048, 1024], P(('samp', 'cent'))
- representative: float32 [2048, 1024], P(('samp', 'cent'))
- keep_weight: float32 [16384], P(('samp', 'cent'))
The draws below stay inside these ranges and needn't reach their ends.
Inputs may be any that keep to these rules, and one draw needn't show every extreme that they name: `owner_map`: every device index, samp-major, owns exactly 64 clusters. `assignment`: of the 512 rows of one device, at most 64 lie in clusters owned by any one device; in every draw some device owns clusters that hold exactly 64 rows of every device.
All inputs are finite; a program needn't handle non-finite values.
Results may differ from the reference program's by a relative error of at most 0.0034.
Values may be sent and summed in bfloat16 or wider, within the bound.
A program may use at most 64 MiB of HBM per device.

```python
import jax
import jax.numpy as jnp
from jax import lax

D = 1024
ROW_DEV = 512
K_DEV = 64
ROWS = 16384
K = 2048
CAP = 64


def shared_layout(key):
    device_count = ROWS // ROW_DEV
    cluster_perm = jax.random.permutation(jax.random.fold_in(key, 11), K)
    owner_values = (cluster_perm // K_DEV).astype(jnp.int32)
    inverse_perm = jnp.argsort(cluster_perm, stable=True).astype(jnp.int32)
    hottest = jax.random.randint(jax.random.fold_in(key, 12), (), 0, device_count)
    block_keys = jax.random.split(jax.random.fold_in(key, 13), device_count)

    def one_block(block_key):
        first_key, second_key, third_key, fourth_key = jax.random.split(block_key, 4)
        other_slots = jax.random.permutation(first_key, (device_count - 1) * CAP)[:ROW_DEV - CAP] // CAP
        other_slots = other_slots + (other_slots >= hottest).astype(jnp.int32)
        targets = jnp.concatenate([jnp.full((CAP,), hottest, jnp.int32), other_slots.astype(jnp.int32)])
        targets = jax.random.permutation(second_key, targets)
        local_rank = jnp.minimum(jax.random.randint(third_key, (ROW_DEV,), 0, K_DEV), jax.random.randint(fourth_key, (ROW_DEV,), 0, K_DEV))
        return inverse_perm[targets * K_DEV + local_rank]
    chosen = jax.vmap(one_block)(block_keys).reshape(ROWS).astype(jnp.int32)
    return (owner_values, chosen)


def draw_owner_map(key, part):
    return shared_layout(key)[0]


def draw_assignment(key, part):
    return shared_layout(key)[1]


def draw_embeddings(key, part):
    chosen = shared_layout(key)[1]
    table = jax.random.normal(jax.random.fold_in(key, 21), (K, D), jnp.float32)
    strength = jax.random.uniform(jax.random.fold_in(key, 22), (ROWS, 1), jnp.float32, 0.3, 3.0)
    noise = jax.random.normal(jax.random.fold_in(key, 23), (ROWS, D), jnp.float32)
    values = strength * table[chosen] + noise
    return jnp.clip(values, -40.0, 40.0)


def setup_inputs(seed: int = 0) -> dict:
    streams_of = jax.random.split(jax.random.key(seed), 4)
    embeddings = draw_embeddings(jax.random.fold_in(streams_of[3], 71), 0)
    assignment = draw_assignment(jax.random.fold_in(streams_of[3], 71), 0)
    owner_map = draw_owner_map(jax.random.fold_in(streams_of[3], 71), 0)
    return {"embeddings": embeddings, "assignment": assignment, "owner_map": owner_map}


EPSILON = 1e-06
SHARPNESS = 8.0

def reference(embeddings, assignment, owner_map):
    unit_rows = (embeddings * lax.rsqrt(lax.optimization_barrier(jnp.sum(embeddings * embeddings, axis=1, keepdims=True)) + EPSILON)).astype(jnp.bfloat16)
    unit_wide = lax.optimization_barrier(unit_rows).astype(jnp.float32)
    cluster_sums = jax.ops.segment_sum(unit_wide, assignment, num_segments=K)
    sum_squares = lax.optimization_barrier(jnp.sum(cluster_sums * cluster_sums, axis=1))
    row_order = jnp.argsort(assignment, stable=True).astype(jnp.int32)
    sorted_units = unit_rows[row_order]
    sorted_ids = assignment[row_order]
    member_counts = jax.ops.segment_sum(jnp.ones((ROWS,), jnp.int32), assignment, num_segments=K).astype(jnp.int32)
    seg_starts = jnp.concatenate([jnp.zeros((1,), jnp.int32), jnp.cumsum(member_counts).astype(jnp.int32)])
    block_size = 128

    def score_block(block_index):
        block_rows = lax.dynamic_slice_in_dim(sorted_units, block_index * block_size, block_size)
        block_ids = lax.dynamic_slice_in_dim(sorted_ids, block_index * block_size, block_size)
        lower_bound = seg_starts[block_ids[0]]
        upper_bound = seg_starts[block_ids[block_size - 1] + 1]
        first_col = (lower_bound // block_size).astype(jnp.int32)
        last_col = ((upper_bound + block_size - 1) // block_size).astype(jnp.int32)

        def column_step(column_index, totals):
            columns = lax.dynamic_slice_in_dim(sorted_units, column_index * block_size, block_size)
            column_ids = lax.dynamic_slice_in_dim(sorted_ids, column_index * block_size, block_size)
            gram = jnp.dot(block_rows, columns.T, preferred_element_type=jnp.float32)
            same_cluster = block_ids[:, None] == column_ids[None, :]
            similar = totals[0] + lax.optimization_barrier(jnp.sum(jnp.where(same_cluster, gram, 0.0), axis=1))
            density = totals[1] + lax.optimization_barrier(jnp.sum(jnp.where(same_cluster, jnp.exp(SHARPNESS * (gram - 1.0)), 0.0), axis=1))
            return (similar, density)
        empty = jnp.zeros((block_size,), jnp.float32)
        return lax.fori_loop(first_col, last_col, column_step, (empty, empty))
    similar, density = lax.map(score_block, jnp.arange(ROWS // block_size, dtype=jnp.int32))
    similar = similar.reshape(ROWS)
    density = density.reshape(ROWS)
    inverse_norm = lax.rsqrt(sum_squares + EPSILON)[sorted_ids]
    spread = 1.0 - similar * inverse_norm
    sorted_weight = jnp.exp(spread) / density
    keep_weight = jnp.zeros((ROWS,), jnp.float32).at[row_order].set(sorted_weight)
    rounded_weight = lax.optimization_barrier(sorted_weight.astype(jnp.bfloat16)).astype(jnp.float32)
    weighted_sums = jax.ops.segment_sum(rounded_weight[:, None] * sorted_units.astype(jnp.float32), sorted_ids, num_segments=K)
    centroid = cluster_sums * lax.rsqrt(sum_squares + EPSILON)[:, None]
    representative = weighted_sums * lax.rsqrt(lax.optimization_barrier(jnp.sum(weighted_sums * weighted_sums, axis=1, keepdims=True)) + EPSILON)
    cluster_order = jnp.argsort(owner_map, stable=True).astype(jnp.int32)
    return (centroid[cluster_order], representative[cluster_order], keep_weight)
```

```python
import functools

import jax
import jax.numpy as jnp
from jax import lax
from jax.experimental import pallas as pl
from jax.experimental.pallas import tpu as pltpu
from jax.sharding import PartitionSpec as P

EPSILON = 1e-06
SHARPNESS = 8.0
LANES = 128
HALF = LANES // 2
SPILL = 65536.0
BF = jnp.bfloat16
F32 = jnp.float32
I32 = jnp.int32
MESH = pl.DeviceIdType.MESH


def iota(shape, axis):
    return lax.broadcasted_iota(jnp.int32, shape, axis)


def row_dot(a, b):
    return lax.dot_general(a, b, (((1,), (1,)), ((), ())), preferred_element_type=F32)


def dot(a, b):
    return jnp.dot(a, b, preferred_element_type=F32)


def column_sum(a):
    return jnp.sum(a, axis=0, keepdims=True)


def loop(low, high, body):
    def step(k, _):
        body(k)
        return 0

    lax.fori_loop(low, high, step, 0)


def flip(index, bits, size):
    if size & (size - 1):
        return (index + bits) % size
    step = 1
    out = index
    while step <= bits:
        if bits & step:
            out = out + step * (1 - 2 * ((index // step) % 2))
        step *= 2
    return out


def dedup_kernel(
    n_samp, n_cent, groups, per_owner, quota, bin_rows, lane_rows,
    emb_hbm, assign_ref, owner_ref, cent_ref, rep_ref, back_ref, meta_ref,
    emb_ref, upper_ref, direct_ref, x_ref, tag_out_ref, tag_ref, bin_out_ref, bin_ref, note_out_ref, note_ref,
    lane_out_ref, lane_ref, mark_out_ref, mark_ref, col_ref, turn_ref, cent_out_ref, rep_out_ref, weight_ref,
    load_sem, own_sem, direct_out, direct_in, tag_out, tag_in, bin_out, bin_in, note_out, note_in,
    lane_out, lane_in, mark_out, mark_in, cent_send, cent_recv, rep_send, rep_recv, weight_out, weight_in,
):
    samp = lax.axis_index("samp")
    cent = lax.axis_index("cent")
    me = samp * n_cent + cent
    devices = n_samp * n_cent
    rows, width = emb_ref.shape
    table_rows = owner_ref.shape[0]
    span = devices // groups
    near = n_cent // groups
    each = per_owner // span
    wide = each * (width // LANES)
    group = cent // near
    mine = samp * near + cent % near
    slots = devices * quota
    late_slots = n_cent * HALF
    held = n_samp * HALF

    def who(index):
        return (index // n_cent, index % n_cent)

    def member(index):
        return (index // near, group * near + index % near)

    def remote(source, target, sent, received, device):
        return pltpu.make_async_remote_copy(
            source, target, sent, received, device_id=device, device_id_type=MESH
        )

    part = rows // load_sem.shape[0]
    loads = [
        pltpu.make_async_copy(
            emb_hbm.at[pl.ds(i * part, part)], emb_ref.at[pl.ds(i * part, part)], load_sem.at[i]
        )
        for i in range(load_sem.shape[0])
    ]
    for copy in loads:
        copy.start()
    barrier = pltpu.get_barrier_semaphore()
    loop(
        1, devices,
        lambda k: pl.semaphore_signal(
            barrier, inc=1, device_id=who((me + k) % devices), device_id_type=MESH
        ),
    )

    bin_ref[:, bin_rows:, :] = jnp.zeros((n_samp, HALF - bin_rows, width), BF)
    lane_ref[:, lane_rows:, :] = jnp.zeros((n_cent, HALF - lane_rows, width), BF)
    upper_ref[...] = (iota(upper_ref.shape, 0) < iota(upper_ref.shape, 1)).astype(BF)

    owner = owner_ref[...]
    owner_hot = (iota((table_rows, devices, LANES), 1) == owner[:, None, :]).astype(F32)
    before = dot(
        owner_hot.reshape(table_rows * devices, LANES).astype(BF), upper_ref[0:LANES, 0:LANES]
    ).reshape(table_rows, devices, LANES)
    base = jnp.zeros((devices, 1), F32)
    ranks = []
    for i in range(table_rows):
        ranks.append(column_sum(owner_hot[i] * (before[i] + base)))
        base = base + jnp.sum(owner_hot[i], axis=1, keepdims=True)
    table = jnp.concatenate([owner.astype(F32)] + ranks, axis=0).astype(BF)
    assign = assign_ref[...]
    found = dot(table, (iota((LANES, rows), 0) == assign % LANES).astype(BF))
    line = iota((table_rows, rows), 0) == assign // LANES
    own = column_sum(jnp.where(line, found[0:table_rows, :], 0.0)).astype(I32)
    rank = column_sum(jnp.where(line, found[table_rows:, :], 0.0)).astype(I32)
    is_high = rank >= per_owner // 2
    fold = jnp.where(is_high, per_owner - 1 - rank, rank)
    place = fold % span
    own_cent = own % n_cent
    to_samp = place // near
    to_cent = (own_cent // near) * near + place % near
    chosen = fold // span + jnp.where(is_high, each // 2, 0)
    tag = (((own // n_cent) * near + own_cent % near) * each + chosen + 1).astype(F32)
    dest = to_samp * n_cent + to_cent

    upper = upper_ref[0:rows, 0:rows]
    dest_hot = (iota((devices, rows), 0) == dest).astype(F32)
    within = column_sum(dest_hot * dot(dest_hot.astype(BF), upper)).astype(I32)
    is_late = within >= quota
    late_hot = ((iota((n_samp, rows), 0) == to_samp) & is_late).astype(F32)
    place = column_sum(late_hot * dot(late_hot.astype(BF), upper)).astype(I32)
    crowded = jnp.max(jnp.where(is_late & (place >= bin_rows), 1.0, 0.0), axis=1, keepdims=True)
    meta_ref[...] = jnp.where(
        iota((8, rows), 0) == 0, dest, jnp.where(is_late, HALF + place, within)
    )

    pack = LANES // quota
    seat = jnp.where(is_late, -1, (me % pack) * quota + within)
    tag_out_ref[:, 0, :] = row_dot(
        (dest_hot * tag).astype(BF), (iota((LANES, rows), 0) == seat).astype(BF)
    )
    seat = jnp.where(is_late & (place < bin_rows), (samp % 2) * HALF + place, -1)
    notes = row_dot(
        jnp.concatenate([late_hot * tag, late_hot * to_cent.astype(F32)], axis=0).astype(BF),
        (iota((LANES, rows), 0) == seat).astype(BF),
    )
    note_out_ref[:, 0, :] = notes[0:n_samp, :] + LANES * notes[n_samp:, :]

    for copy in loads:
        copy.wait()
    emb = emb_ref[...]
    unit = (emb * lax.rsqrt(jnp.sum(emb * emb, axis=1, keepdims=True) + EPSILON)).astype(BF)
    seat = jnp.where(is_late & (place < bin_rows), to_samp * bin_rows + place, -1)
    hot = (iota((n_samp * bin_rows, rows), 0) == seat).astype(BF)
    bin_out_ref[...] = dot(hot, unit).astype(BF).reshape(n_samp, bin_rows, width)
    seat = jnp.where(is_late, -1, dest * quota + within)
    for start in range(0, slots, 2 * LANES):
        hot = (iota((2 * LANES, rows), 0) + start == seat).astype(BF)
        direct_ref[start // quota:(start + 2 * LANES) // quota] = (
            dot(hot, unit).astype(BF).reshape(2 * LANES // quota, quota, width)
        )

    def bin_copy(to, slot):
        return remote(
            bin_out_ref.at[to], bin_ref.at[slot, pl.ds(0, bin_rows)], bin_out.at[to], bin_in.at[slot], (to, cent)
        )

    def note_copy(to, slot):
        return remote(note_out_ref.at[to], note_ref.at[slot], note_out.at[to], note_in.at[slot], (to, cent))

    def direct_copy(to, slot):
        return remote(direct_ref.at[to], x_ref.at[slot], direct_out.at[to], direct_in.at[slot], who(to))

    def tag_copy(to, slot):
        return remote(tag_out_ref.at[to], tag_ref.at[slot], tag_out.at[to], tag_in.at[slot], who(to))

    def lane_copy(to, slot):
        return remote(
            lane_out_ref.at[to, pl.ds(0, lane_rows)], lane_ref.at[slot, pl.ds(0, lane_rows)],
            lane_out.at[to], lane_in.at[slot], (samp, to),
        )

    def mark_copy(to, slot):
        return remote(mark_out_ref.at[to], mark_ref.at[slot], mark_out.at[to], mark_in.at[slot], (samp, to))

    def cent_copy(to, slot):
        return remote(cent_out_ref.at[to], cent_ref.at[slot], cent_send.at[to], cent_recv.at[slot], member(to))

    def rep_copy(to, slot):
        return remote(rep_out_ref.at[to], rep_ref.at[slot], rep_send.at[to], rep_recv.at[slot], member(to))

    def weight_copy(to, slot):
        return remote(weight_ref.at[to], back_ref.at[slot], weight_out.at[to], weight_in.at[slot], who(to))

    def peers(count, index, body):
        loop(1, count, lambda k: body((index + k) % count))

    local = [
        pltpu.make_async_copy(bin_out_ref.at[samp], bin_ref.at[samp, pl.ds(0, bin_rows)], own_sem.at[0]),
        pltpu.make_async_copy(note_out_ref.at[samp], note_ref.at[samp], own_sem.at[1]),
        pltpu.make_async_copy(direct_ref.at[me], x_ref.at[me], own_sem.at[2]),
        pltpu.make_async_copy(tag_out_ref.at[me], tag_ref.at[me], own_sem.at[3]),
    ]
    for copy in local:
        copy.start()
    pl.semaphore_wait(barrier, devices - 1)
    peers(n_samp, samp, lambda to: note_copy(to, samp).start())
    peers(n_samp, samp, lambda to: bin_copy(to, samp).start())
    order = sorted(range(1, n_cent), key=lambda b: (b < n_cent // 2, b)) + [0]
    for b in order:
        to_plane = flip(cent, b, n_cent)
        loop(
            1 if b == 0 else 0, n_samp,
            lambda k: direct_copy(((samp + k) % n_samp) * n_cent + to_plane, me).start(),
        )
    peers(devices, me, lambda to: tag_copy(to, me).start())
    for copy in local:
        copy.wait()

    peers(n_samp, samp, lambda j: note_copy(j, j).wait_recv())
    peers(n_samp, samp, lambda j: bin_copy(j, j).wait_recv())
    code = jnp.concatenate(
        [note_ref[j] + note_ref[j + 1] for j in range(0, n_samp, 2)], axis=1
    ).astype(I32)
    tag = code % LANES
    to_cent = code // LANES
    lane_hot = ((iota((n_cent, held), 0) == to_cent) & (tag > 0)).astype(F32)
    place = column_sum(lane_hot * dot(lane_hot.astype(BF), upper_ref[0:held, 0:held])).astype(I32)
    fits = place < jnp.where(to_cent == cent, HALF, lane_rows)
    crowded = jnp.maximum(
        crowded, jnp.max(jnp.where((tag > 0) & jnp.logical_not(fits), 1.0, 0.0), axis=1, keepdims=True)
    )
    fits = fits & (tag > 0)
    hot = (iota((late_slots, held), 0) == jnp.where(fits, to_cent * HALF + place, -1)).astype(BF)
    lane_out_ref[...] = (
        dot(hot, bin_ref[...].reshape(held, width)).astype(BF).reshape(n_cent, HALF, width)
    )
    which = iota((16, held), 0)
    at = iota((16, held), 1)
    pieces = jnp.where(
        which == 0, tag, jnp.where(which == 1, at % HALF, jnp.where(which == 2, at // HALF, 0))
    ).astype(F32).astype(BF)
    for c in range(n_cent):
        seat = jnp.where(fits & (to_cent == c), (cent % 2) * HALF + place, -1)
        marks = row_dot(pieces, (iota((LANES, held), 0) == seat).astype(BF))
        mark_out_ref[c] = marks[0:1, :] + LANES * (marks[1:2, :] + HALF * marks[2:3, :])
    local = [
        pltpu.make_async_copy(lane_out_ref.at[cent], lane_ref.at[cent], own_sem.at[0]),
        pltpu.make_async_copy(mark_out_ref.at[cent], mark_ref.at[cent], own_sem.at[1]),
    ]
    for copy in local:
        copy.start()
    for b in order[:-1]:
        lane_copy(flip(cent, b, n_cent), cent).start()
    for b in order[:-1]:
        mark_copy(flip(cent, b, n_cent), cent).start()
    for copy in local:
        copy.wait()

    def columns(tags, at):
        for start in range(0, tags.shape[1], LANES):
            chunk = jnp.broadcast_to(tags[:, start:start + LANES], (LANES, LANES))
            col_ref[at + start:at + start + LANES, :] = jnp.transpose(chunk)

    def score(lines, at, fresh, tags):
        gram = row_dot(lines, fresh)
        left = col_ref[at:at + lines.shape[0], :]
        same = jnp.concatenate([left] * (tags.shape[1] // LANES), axis=1) == tags
        near_by = jnp.where(same, jnp.exp(SHARPNESS * (gram - 1.0)), 0.0)
        return column_sum(jnp.where(same, gram, 0.0)), column_sum(near_by)

    peers(devices, me, lambda j: tag_copy(j, j).wait_recv())
    tags = []
    for start in range(0, devices, pack):
        total = tag_ref[start]
        for j in range(start + 1, start + pack):
            total = total + tag_ref[j]
        tags.append(total)
    tags = jnp.concatenate(tags, axis=1)
    columns(tags, 0)
    hits = (iota((per_owner, slots), 0) + 1).astype(F32) == tags
    member_hot = hits.astype(BF)
    peers(devices, me, lambda j: direct_copy(j, j).wait_recv())
    block = 2 * LANES
    step = block // quota
    similar = jnp.zeros((1, slots), F32)
    density = jnp.zeros((1, slots), F32)
    x = x_ref[...].reshape(slots, width)
    for start in range(0, slots, block):
        lines = x_ref[start // quota:start // quota + step].reshape(block, width)
        more = score(lines, start, x, tags)
        similar = similar + more[0]
        density = density + more[1]
    sums = dot(member_hot, x)

    loop(1, n_cent, lambda k: mark_copy((cent + k) % n_cent, (cent + k) % n_cent).wait_recv())
    code = jnp.concatenate(
        [mark_ref[j] + mark_ref[j + 1] for j in range(0, n_cent, 2)], axis=1
    ).astype(I32)
    late_tags = (code % LANES).astype(F32)
    late_at = (code // LANES) % HALF
    late_from = (code // (LANES * HALF)) * n_cent + iota((1, late_slots), 1) // HALF
    columns(late_tags, slots)
    late_hits = (iota((per_owner, late_slots), 0) + 1).astype(F32) == late_tags
    loop(1, n_cent, lambda k: lane_copy((cent + k) % n_cent, (cent + k) % n_cent).wait_recv())
    late = lane_ref[...].reshape(late_slots, width)
    sums = sums + dot(late_hits.astype(BF), late)
    inverse = lax.rsqrt(jnp.sum(sums * sums, axis=1, keepdims=True) + EPSILON)

    def fold_out(value, target):
        for i in range(width // LANES):
            turn_ref[pl.ds(i, per_owner, stride=width // LANES), :] = value[:, i * LANES:(i + 1) * LANES]
        target[...] = turn_ref[...].astype(BF).reshape(span, wide, LANES)

    fold_out(sums * inverse, cent_out_ref)
    peers(span, mine, lambda to: cent_copy(to, mine).start())
    more = score(late, slots, x, tags)
    similar = similar + more[0]
    density = density + more[1]
    late_similar, late_density = score(late, slots, late, late_tags)
    for start in range(0, slots, block):
        lines = x_ref[start // quota:start // quota + step].reshape(block, width)
        more = score(lines, start, late, late_tags)
        late_similar = late_similar + more[0]
        late_density = late_density + more[1]

    def weigh(valid, hit, alike, close):
        scale = column_sum(jnp.where(hit, inverse, 0.0))
        return jnp.where(
            valid, jnp.exp(1.0 - alike * scale) / jnp.where(valid, close, 1.0), 0.0
        )

    weight = weigh(tags > 0.0, hits, similar, density)
    late_weight = weigh(late_tags > 0.0, late_hits, late_similar, late_density)
    mixed = dot(jnp.where(hits, weight, 0.0).astype(BF), x) + dot(
        jnp.where(late_hits, late_weight, 0.0).astype(BF), late
    )
    fold_out(
        mixed * lax.rsqrt(jnp.sum(mixed * mixed, axis=1, keepdims=True) + EPSILON), rep_out_ref
    )
    peers(span, mine, lambda to: rep_copy(to, mine).start())

    def halves(value):
        high = value.astype(BF)
        return jnp.concatenate([high, (value - high.astype(F32)).astype(BF)], axis=0)

    first = jnp.where(iota((devices, slots), 1) // quota == iota((devices, slots), 0), weight, 0.0)
    second = jnp.where(late_from == iota((devices, late_slots), 0), late_weight, 0.0)
    spread = row_dot(
        halves(first), (iota((LANES, slots), 1) % quota == iota((LANES, slots), 0)).astype(BF)
    ) + row_dot(halves(second), (HALF + late_at == iota((LANES, late_slots), 0)).astype(BF))
    flag = jnp.where((iota((1, LANES), 1) == LANES - 1) & (crowded > 0.0), SPILL, 0.0)
    weight_ref[:, 0, :] = spread[0:devices, :] + spread[devices:, :] + flag
    peers(devices, me, lambda to: weight_copy(to, me).start())
    local = [
        pltpu.make_async_copy(cent_out_ref.at[mine], cent_ref.at[mine], own_sem.at[0]),
        pltpu.make_async_copy(rep_out_ref.at[mine], rep_ref.at[mine], own_sem.at[1]),
        pltpu.make_async_copy(weight_ref.at[me], back_ref.at[me], own_sem.at[2]),
    ]
    for copy in local:
        copy.start()

    peers(n_samp, samp, lambda to: note_copy(to, samp).wait_send())
    peers(n_samp, samp, lambda to: bin_copy(to, samp).wait_send())
    peers(devices, me, lambda to: direct_copy(to, me).wait_send())
    peers(devices, me, lambda to: tag_copy(to, me).wait_send())
    peers(n_cent, cent, lambda to: lane_copy(to, cent).wait_send())
    peers(n_cent, cent, lambda to: mark_copy(to, cent).wait_send())
    peers(span, mine, lambda to: cent_copy(to, mine).wait_send())
    peers(span, mine, lambda to: rep_copy(to, mine).wait_send())
    peers(devices, me, lambda to: weight_copy(to, me).wait_send())
    for copy in local:
        copy.wait()
    peers(span, mine, lambda j: cent_copy(j, j).wait_recv())
    peers(span, mine, lambda j: rep_copy(j, j).wait_recv())
    peers(devices, me, lambda j: weight_copy(j, j).wait_recv())


def finish_kernel(
    per_owner, cent_ref, rep_ref, back_ref, meta_ref, centroid_ref, representative_ref, keep_ref, top_ref, turn_ref
):
    span, wide, _ = cent_ref.shape
    each = per_owner // span
    chunks = wide // each
    devices = back_ref.shape[0]
    rows = meta_ref.shape[1]
    back = back_ref[:, 0, :]
    top_ref[0, 0] = jnp.max(back)
    rank = iota((per_owner, per_owner), 0)
    is_high = rank >= per_owner // 2
    fold = jnp.where(is_high, per_owner - 1 - rank, rank)
    source = (fold % span) * each + fold // span + jnp.where(is_high, each // 2, 0)
    order = (iota((per_owner, per_owner), 1) == source).astype(BF)
    for got, out in ((cent_ref, centroid_ref), (rep_ref, representative_ref)):
        turn_ref[...] = got[...].reshape(span * wide, LANES).astype(F32)
        flat = jnp.concatenate(
            [turn_ref[pl.ds(i, per_owner, stride=chunks), :] for i in range(chunks)], axis=1
        )
        out[...] = dot(order, flat.astype(BF))
    meta = meta_ref[...]
    dest_hot = (iota((devices, rows), 0) == meta[0:1, :]).astype(F32)
    spread = lax.dot_general(
        back, dest_hot, (((0,), (0,)), ((), ())),
        preferred_element_type=F32, precision=lax.Precision.HIGHEST,
    )
    hit = iota((LANES, rows), 0) == meta[1:2, :]
    keep_ref[...] = column_sum(jnp.where(hit, spread, 0.0))


def all_pairs(arrived, arrived_tags, validity, block_size):
    slot_count, feature_width = arrived.shape
    block_count = slot_count // block_size

    def score_block(pieces):
        block_rows, block_tags = pieces
        gram = jnp.einsum("rd,qd->rq", block_rows, arrived, preferred_element_type=jnp.float32)
        same_cluster = (block_tags[:, None] == arrived_tags[None, :]) & validity[None, :]
        similar = jnp.sum(jnp.where(same_cluster, gram, 0.0), axis=1)
        density = jnp.sum(jnp.where(same_cluster, jnp.exp(SHARPNESS * (gram - 1.0)), 0.0), axis=1)
        return (similar, density)

    similar, density = lax.map(
        score_block,
        (
            arrived.reshape(block_count, block_size, feature_width),
            arrived_tags.reshape(block_count, block_size),
        ),
    )
    return (similar.reshape(slot_count), density.reshape(slot_count))


def full_capacity(embeddings, assignment, owner_map):
    row_count, feature_width = embeddings.shape
    devices = lax.axis_size("samp") * lax.axis_size("cent")
    clusters = owner_map.shape[0]
    per_owner = clusters // devices
    capacity = 4 * row_count // devices
    slot_count = devices * capacity
    unit_rows = (
        embeddings * lax.rsqrt(jnp.sum(embeddings * embeddings, axis=1, keepdims=True) + EPSILON)
    ).astype(jnp.bfloat16)
    destination = owner_map[assignment]
    cluster_order = jnp.argsort(owner_map, stable=True)
    position = (
        jnp.zeros((clusters,), jnp.int32)
        .at[cluster_order]
        .set(jnp.arange(clusters, dtype=jnp.int32))
    )
    local_rank = position[assignment] - destination * per_owner
    dest_onehot = (destination[:, None] == jnp.arange(devices, dtype=jnp.int32)[None, :]).astype(
        jnp.int32
    )
    within_rank = jnp.sum(jnp.cumsum(dest_onehot, axis=0) * dest_onehot, axis=1) - 1
    slot_index = destination * capacity + within_rank
    outgoing = jnp.zeros((slot_count, feature_width), jnp.bfloat16).at[slot_index].set(unit_rows)
    labels = (
        jnp.zeros((slot_count,), jnp.bfloat16)
        .at[slot_index]
        .set((local_rank + 1).astype(jnp.bfloat16))
    )
    arrived, arrived_labels = (
        lax.all_to_all(outgoing, ("samp", "cent"), split_axis=0, concat_axis=0, tiled=True),
        lax.all_to_all(labels, ("samp", "cent"), split_axis=0, concat_axis=0, tiled=True),
    )
    arrived_tags = arrived_labels.astype(jnp.int32) - 1
    validity = arrived_tags >= 0
    block_size = min(512, slot_count)
    similar, density = all_pairs(arrived, arrived_tags, validity, block_size)
    member = arrived_tags[None, :] == jnp.arange(per_owner, dtype=jnp.int32)[:, None]
    member_bf = member.astype(jnp.bfloat16)
    cluster_sums = jnp.dot(member_bf, arrived, preferred_element_type=jnp.float32)
    inverse_norm = lax.rsqrt(jnp.sum(cluster_sums * cluster_sums, axis=1) + EPSILON)
    row_scale = jnp.sum(member.astype(jnp.float32) * inverse_norm[:, None], axis=0)
    spread = 1.0 - similar * row_scale
    weight = jnp.where(validity, jnp.exp(spread) / jnp.where(validity, density, 1.0), 0.0)
    weighted = jnp.dot(
        member_bf * weight.astype(jnp.bfloat16)[None, :],
        arrived,
        preferred_element_type=jnp.float32,
    )
    centroid = cluster_sums * inverse_norm[:, None]
    representative = weighted * lax.rsqrt(
        jnp.sum(weighted * weighted, axis=1, keepdims=True) + EPSILON
    )
    returned = lax.all_to_all(weight, ("samp", "cent"), split_axis=0, concat_axis=0, tiled=True)
    keep_weight = returned[slot_index]
    return (centroid, representative, keep_weight)


def on_device(embeddings, assignment, owner_map):
    rows, width = embeddings.shape
    n_samp = lax.axis_size("samp")
    n_cent = lax.axis_size("cent")
    devices = n_samp * n_cent
    clusters = owner_map.shape[0]
    per_owner = clusters // devices
    groups = max(1, 2 * devices // per_owner)
    quota = -(-rows // devices // 16) * 16
    bin_rows = 48
    lane_rows = 56
    span = devices // groups
    wide = per_owner // span * (width // LANES)
    slots = devices * quota
    late_slots = n_cent * HALF
    depth = max(rows, n_samp * HALF)
    vmem = pl.BlockSpec(memory_space=pltpu.VMEM)
    anywhere = pl.BlockSpec(memory_space=pl.ANY)
    shape = jax.ShapeDtypeStruct
    dma = pltpu.SemaphoreType.DMA
    centroid, representative, back, meta = pl.pallas_call(
        functools.partial(
            dedup_kernel, n_samp, n_cent, groups, per_owner, quota, bin_rows, lane_rows
        ),
        out_shape=(
            shape((span, wide, LANES), BF),
            shape((span, wide, LANES), BF),
            shape((devices, 1, LANES), F32),
            shape((8, rows), I32),
        ),
        in_specs=[anywhere, vmem, vmem],
        out_specs=(vmem,) * 4,
        scratch_shapes=[
            pltpu.VMEM((rows, width), F32),
            pltpu.VMEM((depth, depth), BF),
            pltpu.VMEM((devices, quota, width), BF),
            pltpu.VMEM((devices, quota, width), BF),
            pltpu.VMEM((devices, 1, LANES), F32),
            pltpu.VMEM((devices, 1, LANES), F32),
            pltpu.VMEM((n_samp, bin_rows, width), BF),
            pltpu.VMEM((n_samp, HALF, width), BF),
            pltpu.VMEM((n_samp, 1, LANES), F32),
            pltpu.VMEM((n_samp, 1, LANES), F32),
            pltpu.VMEM((n_cent, HALF, width), BF),
            pltpu.VMEM((n_cent, HALF, width), BF),
            pltpu.VMEM((n_cent, 1, LANES), F32),
            pltpu.VMEM((n_cent, 1, LANES), F32),
            pltpu.VMEM((slots + late_slots, LANES), F32),
            pltpu.VMEM((span * wide, LANES), F32),
            pltpu.VMEM((span, wide, LANES), BF),
            pltpu.VMEM((span, wide, LANES), BF),
            pltpu.VMEM((devices, 1, LANES), F32),
            dma((4,)), dma((4,)),
            dma((devices,)), dma((devices,)), dma((devices,)), dma((devices,)),
            dma((n_samp,)), dma((n_samp,)), dma((n_samp,)), dma((n_samp,)),
            dma((n_cent,)), dma((n_cent,)), dma((n_cent,)), dma((n_cent,)),
            dma((span,)), dma((span,)), dma((span,)), dma((span,)),
            dma((devices,)), dma((devices,)),
        ],
        compiler_params=pltpu.CompilerParams(collective_id=0, has_side_effects=True),
        name="dedup",
    )(embeddings, assignment.reshape(1, rows), owner_map.reshape(clusters // LANES, LANES))
    centroid, representative, keep, top = pl.pallas_call(
        functools.partial(finish_kernel, per_owner),
        out_shape=(
            shape((per_owner, width), F32),
            shape((per_owner, width), F32),
            shape((1, rows), F32),
            shape((1, 1), F32),
        ),
        in_specs=[vmem] * 4,
        out_specs=(vmem, vmem, vmem, pl.BlockSpec(memory_space=pltpu.SMEM)),
        scratch_shapes=[pltpu.VMEM((span * wide, LANES), F32)],
        name="finish",
    )(centroid, representative, back, meta)
    keep = keep.reshape(rows)

    def fast(embeddings, assignment, owner_map, centroid, representative, keep):
        return centroid, representative, keep

    def slow(embeddings, assignment, owner_map, centroid, representative, keep):
        return full_capacity(embeddings, assignment, owner_map)

    spilled = top[0, 0] >= SPILL
    return lax.cond(
        spilled, slow, fast, embeddings, assignment, owner_map, centroid, representative, keep
    )


def solution(mesh):
    in_specs = (P(("samp", "cent"), None), P(("samp", "cent")), P())
    out_specs = (P(("samp", "cent"), None), P(("samp", "cent"), None), P(("samp", "cent")))
    return jax.shard_map(
        on_device, mesh=mesh, in_specs=in_specs, out_specs=out_specs, check_vma=False
    )
```

```python
import functools

import jax
import jax.numpy as jnp
from jax import lax
from jax.experimental import pallas as pl
from jax.experimental.pallas import tpu as pltpu
from jax.sharding import PartitionSpec as P

EPSILON = 1e-06
SHARPNESS = 8.0
LANES = 128
HALF = LANES // 2
SPILL = 65536.0
BF = jnp.bfloat16
F32 = jnp.float32
I32 = jnp.int32
MESH = pl.DeviceIdType.MESH


def iota(shape, axis):
    return lax.broadcasted_iota(jnp.int32, shape, axis)


def row_dot(a, b):
    return lax.dot_general(a, b, (((1,), (1,)), ((), ())), preferred_element_type=F32)


def dot(a, b):
    return jnp.dot(a, b, preferred_element_type=F32)


def column_sum(a):
    return jnp.sum(a, axis=0, keepdims=True)


def flip(index, bits):
    step = 1
    while step <= bits:
        if bits & step:
            index = index + step * (1 - 2 * ((index // step) % 2))
        step *= 2
    return index


def plane_order(n_cent):
    return sorted(range(1, n_cent), key=lambda b: (b < n_cent // 2, b)) + [0]


def dedup_kernel(
    n_samp, n_cent, groups, per_owner, quota, bin_rows, lane_rows,
    emb_hbm, assign_ref, owner_ref, cent_ref, rep_ref, back_ref, meta_ref,
    emb_ref, upper_ref, direct_ref, x_ref, tag_out_ref, tag_ref, bin_out_ref, bin_ref, note_out_ref, note_ref,
    lane_out_ref, mark_out_ref, mark_ref, col_ref, turn_ref, cent_out_ref, rep_out_ref, weight_ref,
    load_sem, own_sem, direct_out, direct_in, tag_out, tag_in, bin_out, bin_in, note_out, note_in,
    lane_out, lane_in, mark_out, mark_in, cent_send, cent_recv, rep_send, rep_recv, weight_out, weight_in,
):
    samp = lax.axis_index("samp")
    cent = lax.axis_index("cent")
    devices = n_samp * n_cent
    rows, width = emb_ref.shape
    table_rows = owner_ref.shape[0]
    span = devices // groups
    near = n_cent // groups
    each = per_owner // span
    wide = each * (width // LANES)
    slots = devices * quota
    late_slots = n_cent * HALF
    held = n_samp * HALF
    order = plane_order(n_cent)
    samps = [flip(samp, a) for a in range(n_samp)]
    cents = [flip(cent, b) for b in range(n_cent)]
    peers = [
        (i * n_samp + a, (samps[a], cents[b]))
        for i, b in enumerate(order)
        for a in range(n_samp)
        if a or b
    ]
    own = order.index(0) * n_samp

    def remote(source, target, sent, received, device):
        return pltpu.make_async_remote_copy(
            source, target, sent, received, device_id=device, device_id_type=MESH
        )

    part = rows // load_sem.shape[0]
    loads = [
        pltpu.make_async_copy(
            emb_hbm.at[pl.ds(i * part, part)], emb_ref.at[pl.ds(i * part, part)], load_sem.at[i]
        )
        for i in range(load_sem.shape[0])
    ]
    for copy in loads:
        copy.start()
    barrier = pltpu.get_barrier_semaphore()
    for _, device in peers:
        pl.semaphore_signal(barrier, inc=1, device_id=device, device_id_type=MESH)

    bin_ref[:, bin_rows:, :] = jnp.zeros((n_samp, HALF - bin_rows, width), BF)
    for b in range(1, n_cent):
        x_ref[slots + b * HALF + lane_rows:slots + (b + 1) * HALF, :] = jnp.zeros(
            (HALF - lane_rows, width), BF
        )
    upper_ref[...] = (iota(upper_ref.shape, 0) < iota(upper_ref.shape, 1)).astype(BF)

    owner = owner_ref[...]
    owner_hot = (iota((table_rows, devices, LANES), 1) == owner[:, None, :]).astype(F32)
    before = dot(
        owner_hot.reshape(table_rows * devices, LANES).astype(BF), upper_ref[0:LANES, 0:LANES]
    ).reshape(table_rows, devices, LANES)
    base = jnp.zeros((devices, 1), F32)
    ranks = []
    for i in range(table_rows):
        ranks.append(column_sum(owner_hot[i] * (before[i] + base)))
        base = base + jnp.sum(owner_hot[i], axis=1, keepdims=True)
    table = jnp.concatenate([owner.astype(F32)] + ranks, axis=0).astype(BF)
    assign = assign_ref[...]
    found = dot(table, (iota((LANES, rows), 0) == assign % LANES).astype(BF))
    line = iota((table_rows, rows), 0) == assign // LANES
    owned = column_sum(jnp.where(line, found[0:table_rows, :], 0.0)).astype(I32)
    rank = column_sum(jnp.where(line, found[table_rows:, :], 0.0)).astype(I32)
    is_high = rank >= per_owner // 2
    fold = jnp.where(is_high, per_owner - 1 - rank, rank)
    place = fold % span
    own_cent = owned % n_cent
    to_samp = place // near
    to_cent = (own_cent // near) * near + place % near
    chosen = fold // span + jnp.where(is_high, each // 2, 0)
    apart = ((owned // n_cent) ^ to_samp) * near + (own_cent ^ to_cent)
    tag = (apart * each + chosen + 1).astype(F32)
    to_samp = to_samp ^ samp
    to_cent = to_cent ^ cent
    dest = to_samp
    for i, b in enumerate(order):
        dest = dest + jnp.where(to_cent == b, i * n_samp, 0)

    upper = upper_ref[0:rows, 0:rows]
    dest_hot = (iota((devices, rows), 0) == dest).astype(F32)
    within = column_sum(dest_hot * dot(dest_hot.astype(BF), upper)).astype(I32)
    is_late = within >= quota
    late_hot = ((iota((n_samp, rows), 0) == to_samp) & is_late).astype(F32)
    place = column_sum(late_hot * dot(late_hot.astype(BF), upper)).astype(I32)
    crowded = jnp.max(jnp.where(is_late & (place >= bin_rows), 1.0, 0.0), axis=1, keepdims=True)
    meta_ref[...] = jnp.where(
        iota((8, rows), 0) == 0, dest, jnp.where(is_late, HALF + place, within)
    )

    for copy in loads:
        copy.wait()
    emb = emb_ref[...]
    unit = (emb * lax.rsqrt(jnp.sum(emb * emb, axis=1, keepdims=True) + EPSILON)).astype(BF)
    direct_seat = jnp.where(is_late, -1, dest * quota + within)
    block = 2 * LANES

    def pack_direct(start):
        hot = (iota((block, rows), 0) + start == direct_seat).astype(BF)
        direct_ref[start:start + block, :] = dot(hot, unit).astype(BF)

    def direct_copy(slot, device):
        at = pl.ds(slot * quota, quota)
        return remote(direct_ref.at[at], x_ref.at[at], direct_out.at[slot], direct_in.at[slot], device)

    def tag_copy(slot, device):
        return remote(tag_out_ref.at[slot], tag_ref.at[slot], tag_out.at[slot], tag_in.at[slot], device)

    def bin_copy(a):
        return remote(
            bin_out_ref.at[a], bin_ref.at[a, pl.ds(0, bin_rows)], bin_out.at[a], bin_in.at[a], (samps[a], cent)
        )

    def note_copy(a):
        return remote(note_out_ref.at[a], note_ref.at[a], note_out.at[a], note_in.at[a], (samps[a], cent))

    def lane_copy(b):
        return remote(
            lane_out_ref.at[b, pl.ds(0, lane_rows)], x_ref.at[pl.ds(slots + b * HALF, lane_rows)],
            lane_out.at[b], lane_in.at[b], (samp, cents[b]),
        )

    def mark_copy(b):
        return remote(mark_out_ref.at[b], mark_ref.at[b], mark_out.at[b], mark_in.at[b], (samp, cents[b]))

    def cent_copy(slot, device):
        return remote(cent_out_ref.at[slot], cent_ref.at[slot], cent_send.at[slot], cent_recv.at[slot], device)

    def rep_copy(slot, device):
        return remote(rep_out_ref.at[slot], rep_ref.at[slot], rep_send.at[slot], rep_recv.at[slot], device)

    def weight_copy(slot, device):
        return remote(weight_ref.at[slot], back_ref.at[slot], weight_out.at[slot], weight_in.at[slot], device)

    owners = [
        (a * near + b, (samps[a], cents[b]))
        for b in sorted(range(near), key=lambda b: (b < near // 2, b))
        for a in range(n_samp)
        if a or b
    ]

    def send_direct(start):
        for slot, device in peers:
            if start <= slot * quota < start + block:
                direct_copy(slot, device).start()

    pack_direct(0)
    pl.semaphore_wait(barrier, devices - 1)
    send_direct(0)

    seat = jnp.where(is_late & (place < bin_rows), (to_samp % 2) * HALF + place, -1)
    notes = row_dot(
        jnp.concatenate([late_hot * tag, late_hot * to_cent.astype(F32)], axis=0).astype(BF),
        (iota((LANES, rows), 0) == seat).astype(BF),
    )
    note_out_ref[:, 0, :] = notes[0:n_samp, :] + LANES * notes[n_samp:, :]
    seat = jnp.where(is_late & (place < bin_rows), to_samp * bin_rows + place, -1)
    hot = (iota((n_samp * bin_rows, rows), 0) == seat).astype(BF)
    bin_out_ref[...] = dot(hot, unit).astype(BF).reshape(n_samp, bin_rows, width)
    for a in range(1, n_samp):
        note_copy(a).start()
    for a in range(1, n_samp):
        bin_copy(a).start()
    for start in range(block, slots, block):
        pack_direct(start)
        send_direct(start)
    pack = LANES // quota
    seat = jnp.where(is_late, -1, (dest % pack) * quota + within)
    tag_out_ref[:, 0, :] = row_dot(
        (dest_hot * tag).astype(BF), (iota((LANES, rows), 0) == seat).astype(BF)
    )
    for slot, device in peers:
        tag_copy(slot, device).start()
    mine = pl.ds(own * quota, quota)
    local = [
        pltpu.make_async_copy(bin_out_ref.at[0], bin_ref.at[0, pl.ds(0, bin_rows)], own_sem.at[0]),
        pltpu.make_async_copy(note_out_ref.at[0], note_ref.at[0], own_sem.at[1]),
        pltpu.make_async_copy(direct_ref.at[mine], x_ref.at[mine], own_sem.at[2]),
        pltpu.make_async_copy(tag_out_ref.at[own], tag_ref.at[own], own_sem.at[3]),
    ]
    for copy in local:
        copy.start()
    for copy in local:
        copy.wait()

    for a in range(1, n_samp):
        note_copy(a).wait_recv()
    code = jnp.concatenate(
        [note_ref[j] + note_ref[j + 1] for j in range(0, n_samp, 2)], axis=1
    ).astype(I32)
    tag = code % LANES
    to_cent = code // LANES
    lane_hot = ((iota((n_cent, held), 0) == to_cent) & (tag > 0)).astype(F32)
    place = column_sum(lane_hot * dot(lane_hot.astype(BF), upper_ref[0:held, 0:held])).astype(I32)
    fits = place < jnp.where(to_cent == 0, HALF, lane_rows)
    crowded = jnp.maximum(
        crowded, jnp.max(jnp.where((tag > 0) & jnp.logical_not(fits), 1.0, 0.0), axis=1, keepdims=True)
    )
    fits = fits & (tag > 0)
    which = iota((16, held), 0)
    at = iota((16, held), 1)
    pieces = jnp.where(
        which == 0, tag, jnp.where(which == 1, at % HALF, jnp.where(which == 2, at // HALF, 0))
    ).astype(F32).astype(BF)
    for b in range(n_cent):
        seat = jnp.where(fits & (to_cent == b), (b % 2) * HALF + place, -1)
        marks = row_dot(pieces, (iota((LANES, held), 0) == seat).astype(BF))
        mark_out_ref[b] = marks[0:1, :] + LANES * (marks[1:2, :] + HALF * marks[2:3, :])
    hot = (iota((late_slots, held), 0) == jnp.where(fits, to_cent * HALF + place, -1)).astype(BF)
    for a in range(1, n_samp):
        bin_copy(a).wait_recv()
    lane_out_ref[...] = (
        dot(hot, bin_ref[...].reshape(held, width)).astype(BF).reshape(n_cent, HALF, width)
    )
    for b in order[:-1]:
        mark_copy(b).start()
    for b in order[:-1]:
        lane_copy(b).start()
    local = [
        pltpu.make_async_copy(lane_out_ref.at[0], x_ref.at[pl.ds(slots, HALF)], own_sem.at[0]),
        pltpu.make_async_copy(mark_out_ref.at[0], mark_ref.at[0], own_sem.at[1]),
    ]
    for copy in local:
        copy.start()
    for copy in local:
        copy.wait()

    def columns(tags, at):
        for start in range(0, tags.shape[1], LANES):
            chunk = jnp.broadcast_to(tags[:, start:start + LANES], (LANES, LANES))
            col_ref[at + start:at + start + LANES, :] = jnp.transpose(chunk)

    def score(low, high, fresh, tags):
        alike = jnp.zeros(tags.shape, F32)
        close = jnp.zeros(tags.shape, F32)
        for start in range(low, high, block):
            end = min(start + block, high)
            gram = row_dot(x_ref[start:end, :], fresh)
            left = col_ref[start:end, :]
            same = jnp.concatenate([left] * (tags.shape[1] // LANES), axis=1) == tags
            alike = alike + column_sum(jnp.where(same, gram, 0.0))
            close = close + column_sum(jnp.where(same, jnp.exp(SHARPNESS * (gram - 1.0)), 0.0))
        return alike, close

    def hit(tags):
        return (iota((per_owner, tags.shape[1]), 0) + 1).astype(F32) == tags

    for slot, device in peers:
        tag_copy(slot, device).wait_recv()
    tags = []
    for start in range(0, devices, pack):
        total = tag_ref[start]
        for j in range(start + 1, start + pack):
            total = total + tag_ref[j]
        tags.append(total)
    tags = jnp.concatenate(tags, axis=1)
    columns(tags, 0)
    for slot, device in peers:
        direct_copy(slot, device).wait_recv()
    x = x_ref[0:slots, :]
    similar, density = score(0, slots, x, tags)
    sums = dot(hit(tags).astype(BF), x)

    for b in range(1, n_cent):
        mark_copy(b).wait_recv()
    sources = []
    columns_of = []
    for b in range(0, n_cent, 2):
        code = (mark_ref[b] + mark_ref[b + 1]).astype(I32)
        fresh_tags = (code % LANES).astype(F32)
        columns_of.append(HALF + (code // LANES) % HALF)
        lane = iota((1, LANES), 1)
        sources.append(
            code // (LANES * HALF)
            + n_samp * jnp.where(lane < HALF, order.index(b), order.index(b + 1))
        )
        at = slots + b * HALF
        columns(fresh_tags, at)
        for c in (b, b + 1):
            if c:
                lane_copy(c).wait_recv()
        fresh = x_ref[at:at + LANES, :]
        sums = sums + dot(hit(fresh_tags).astype(BF), fresh)
        if b == n_cent - 2:
            inverse = lax.rsqrt(jnp.sum(sums * sums, axis=1, keepdims=True) + EPSILON)
        alike, close = score(0, at + LANES, fresh, fresh_tags)
        more_alike, more_close = score(at, at + LANES, x_ref[0:at, :], tags)
        similar = jnp.concatenate([similar + more_alike, alike], axis=1)
        density = jnp.concatenate([density + more_close, close], axis=1)
        tags = jnp.concatenate([tags, fresh_tags], axis=1)

    def fold_out(value, target):
        for i in range(width // LANES):
            turn_ref[pl.ds(i, per_owner, stride=width // LANES), :] = value[:, i * LANES:(i + 1) * LANES]
        target[...] = turn_ref[...].astype(BF).reshape(span, wide, LANES)

    fold_out(sums * inverse, cent_out_ref)
    for slot, device in owners:
        cent_copy(slot, device).start()
    hits = hit(tags)
    valid = tags > 0.0
    scale = column_sum(jnp.where(hits, inverse, 0.0))
    weight = jnp.where(
        valid, jnp.exp(1.0 - similar * scale) / jnp.where(valid, density, 1.0), 0.0
    )
    mixed = dot(jnp.where(hits, weight, 0.0).astype(BF), x_ref[...])
    fold_out(
        mixed * lax.rsqrt(jnp.sum(mixed * mixed, axis=1, keepdims=True) + EPSILON), rep_out_ref
    )
    for slot, device in owners:
        rep_copy(slot, device).start()

    lane = iota((1, slots), 1)
    sources = jnp.concatenate([lane // quota] + sources, axis=1)
    columns_of = jnp.concatenate([lane % quota] + columns_of, axis=1)
    spread = jnp.where(iota((devices, slots + late_slots), 0) == sources, weight, 0.0)
    high = spread.astype(BF)
    spread = row_dot(
        jnp.concatenate([high, (spread - high.astype(F32)).astype(BF)], axis=0),
        (iota((LANES, slots + late_slots), 0) == columns_of).astype(BF),
    )
    flag = jnp.where((iota((1, LANES), 1) == LANES - 1) & (crowded > 0.0), SPILL, 0.0)
    weight_ref[:, 0, :] = spread[0:devices, :] + spread[devices:, :] + flag
    for slot, device in peers:
        weight_copy(slot, device).start()
    local = [
        pltpu.make_async_copy(cent_out_ref.at[0], cent_ref.at[0], own_sem.at[0]),
        pltpu.make_async_copy(rep_out_ref.at[0], rep_ref.at[0], own_sem.at[1]),
        pltpu.make_async_copy(weight_ref.at[own], back_ref.at[own], own_sem.at[2]),
    ]
    for copy in local:
        copy.start()

    for a in range(1, n_samp):
        note_copy(a).wait_send()
        bin_copy(a).wait_send()
    for b in range(1, n_cent):
        lane_copy(b).wait_send()
        mark_copy(b).wait_send()
    for slot, device in peers:
        direct_copy(slot, device).wait_send()
        tag_copy(slot, device).wait_send()
    for copy in local:
        copy.wait()
    for slot, device in owners:
        cent_copy(slot, device).wait()
        rep_copy(slot, device).wait()
    for slot, device in peers:
        weight_copy(slot, device).wait()


def finish_kernel(
    per_owner, n_cent, cent_ref, rep_ref, back_ref, meta_ref, centroid_ref, representative_ref, keep_ref, top_ref, turn_ref
):
    span, wide, _ = cent_ref.shape
    each = per_owner // span
    chunks = wide // each
    devices = back_ref.shape[0]
    rows = meta_ref.shape[1]
    near = n_cent * span // devices
    mine = lax.axis_index("samp") * near + lax.axis_index("cent") % near
    back = back_ref[:, 0, :]
    top_ref[0, 0] = jnp.max(back)
    rank = iota((per_owner, per_owner), 0)
    is_high = rank >= per_owner // 2
    fold = jnp.where(is_high, per_owner - 1 - rank, rank)
    source = ((fold % span) ^ mine) * each + fold // span + jnp.where(is_high, each // 2, 0)
    order = (iota((per_owner, per_owner), 1) == source).astype(BF)
    for got, out in ((cent_ref, centroid_ref), (rep_ref, representative_ref)):
        turn_ref[...] = got[...].reshape(span * wide, LANES).astype(F32)
        flat = jnp.concatenate(
            [turn_ref[pl.ds(i, per_owner, stride=chunks), :] for i in range(chunks)], axis=1
        )
        out[...] = dot(order, flat.astype(BF))
    meta = meta_ref[...]
    dest_hot = (iota((devices, rows), 0) == meta[0:1, :]).astype(F32)
    spread = lax.dot_general(
        back, dest_hot, (((0,), (0,)), ((), ())),
        preferred_element_type=F32, precision=lax.Precision.HIGHEST,
    )
    hit = iota((LANES, rows), 0) == meta[1:2, :]
    keep_ref[...] = column_sum(jnp.where(hit, spread, 0.0))


def all_pairs(arrived, arrived_tags, validity, block_size):
    slot_count, feature_width = arrived.shape
    block_count = slot_count // block_size

    def score_block(pieces):
        block_rows, block_tags = pieces
        gram = jnp.einsum("rd,qd->rq", block_rows, arrived, preferred_element_type=jnp.float32)
        same_cluster = (block_tags[:, None] == arrived_tags[None, :]) & validity[None, :]
        similar = jnp.sum(jnp.where(same_cluster, gram, 0.0), axis=1)
        density = jnp.sum(jnp.where(same_cluster, jnp.exp(SHARPNESS * (gram - 1.0)), 0.0), axis=1)
        return (similar, density)

    similar, density = lax.map(
        score_block,
        (
            arrived.reshape(block_count, block_size, feature_width),
            arrived_tags.reshape(block_count, block_size),
        ),
    )
    return (similar.reshape(slot_count), density.reshape(slot_count))


def full_capacity(embeddings, assignment, owner_map):
    row_count, feature_width = embeddings.shape
    devices = lax.axis_size("samp") * lax.axis_size("cent")
    clusters = owner_map.shape[0]
    per_owner = clusters // devices
    capacity = 4 * row_count // devices
    slot_count = devices * capacity
    unit_rows = (
        embeddings * lax.rsqrt(jnp.sum(embeddings * embeddings, axis=1, keepdims=True) + EPSILON)
    ).astype(jnp.bfloat16)
    destination = owner_map[assignment]
    cluster_order = jnp.argsort(owner_map, stable=True)
    position = (
        jnp.zeros((clusters,), jnp.int32)
        .at[cluster_order]
        .set(jnp.arange(clusters, dtype=jnp.int32))
    )
    local_rank = position[assignment] - destination * per_owner
    dest_onehot = (destination[:, None] == jnp.arange(devices, dtype=jnp.int32)[None, :]).astype(
        jnp.int32
    )
    within_rank = jnp.sum(jnp.cumsum(dest_onehot, axis=0) * dest_onehot, axis=1) - 1
    slot_index = destination * capacity + within_rank
    outgoing = jnp.zeros((slot_count, feature_width), jnp.bfloat16).at[slot_index].set(unit_rows)
    labels = (
        jnp.zeros((slot_count,), jnp.bfloat16)
        .at[slot_index]
        .set((local_rank + 1).astype(jnp.bfloat16))
    )
    arrived, arrived_labels = (
        lax.all_to_all(outgoing, ("samp", "cent"), split_axis=0, concat_axis=0, tiled=True),
        lax.all_to_all(labels, ("samp", "cent"), split_axis=0, concat_axis=0, tiled=True),
    )
    arrived_tags = arrived_labels.astype(jnp.int32) - 1
    validity = arrived_tags >= 0
    block_size = min(512, slot_count)
    similar, density = all_pairs(arrived, arrived_tags, validity, block_size)
    member = arrived_tags[None, :] == jnp.arange(per_owner, dtype=jnp.int32)[:, None]
    member_bf = member.astype(jnp.bfloat16)
    cluster_sums = jnp.dot(member_bf, arrived, preferred_element_type=jnp.float32)
    inverse_norm = lax.rsqrt(jnp.sum(cluster_sums * cluster_sums, axis=1) + EPSILON)
    row_scale = jnp.sum(member.astype(jnp.float32) * inverse_norm[:, None], axis=0)
    spread = 1.0 - similar * row_scale
    weight = jnp.where(validity, jnp.exp(spread) / jnp.where(validity, density, 1.0), 0.0)
    weighted = jnp.dot(
        member_bf * weight.astype(jnp.bfloat16)[None, :],
        arrived,
        preferred_element_type=jnp.float32,
    )
    centroid = cluster_sums * inverse_norm[:, None]
    representative = weighted * lax.rsqrt(
        jnp.sum(weighted * weighted, axis=1, keepdims=True) + EPSILON
    )
    returned = lax.all_to_all(weight, ("samp", "cent"), split_axis=0, concat_axis=0, tiled=True)
    keep_weight = returned[slot_index]
    return (centroid, representative, keep_weight)


def on_device(embeddings, assignment, owner_map):
    rows, width = embeddings.shape
    n_samp = lax.axis_size("samp")
    n_cent = lax.axis_size("cent")
    devices = n_samp * n_cent
    clusters = owner_map.shape[0]
    per_owner = clusters // devices
    groups = max(1, 2 * devices // per_owner)
    quota = -(-rows // devices // 16) * 16
    bin_rows = 48
    lane_rows = 56
    span = devices // groups
    wide = per_owner // span * (width // LANES)
    slots = devices * quota
    late_slots = n_cent * HALF
    depth = max(rows, n_samp * HALF)
    vmem = pl.BlockSpec(memory_space=pltpu.VMEM)
    anywhere = pl.BlockSpec(memory_space=pl.ANY)
    shape = jax.ShapeDtypeStruct
    dma = pltpu.SemaphoreType.DMA
    centroid, representative, back, meta = pl.pallas_call(
        functools.partial(
            dedup_kernel, n_samp, n_cent, groups, per_owner, quota, bin_rows, lane_rows
        ),
        out_shape=(
            shape((span, wide, LANES), BF),
            shape((span, wide, LANES), BF),
            shape((devices, 1, LANES), F32),
            shape((8, rows), I32),
        ),
        in_specs=[anywhere, vmem, vmem],
        out_specs=(vmem,) * 4,
        scratch_shapes=[
            pltpu.VMEM((rows, width), F32),
            pltpu.VMEM((depth, depth), BF),
            pltpu.VMEM((slots, width), BF),
            pltpu.VMEM((slots + late_slots, width), BF),
            pltpu.VMEM((devices, 1, LANES), F32),
            pltpu.VMEM((devices, 1, LANES), F32),
            pltpu.VMEM((n_samp, bin_rows, width), BF),
            pltpu.VMEM((n_samp, HALF, width), BF),
            pltpu.VMEM((n_samp, 1, LANES), F32),
            pltpu.VMEM((n_samp, 1, LANES), F32),
            pltpu.VMEM((n_cent, HALF, width), BF),
            pltpu.VMEM((n_cent, 1, LANES), F32),
            pltpu.VMEM((n_cent, 1, LANES), F32),
            pltpu.VMEM((slots + late_slots, LANES), F32),
            pltpu.VMEM((span * wide, LANES), F32),
            pltpu.VMEM((span, wide, LANES), BF),
            pltpu.VMEM((span, wide, LANES), BF),
            pltpu.VMEM((devices, 1, LANES), F32),
            dma((4,)), dma((4,)),
            dma((devices,)), dma((devices,)), dma((devices,)), dma((devices,)),
            dma((n_samp,)), dma((n_samp,)), dma((n_samp,)), dma((n_samp,)),
            dma((n_cent,)), dma((n_cent,)), dma((n_cent,)), dma((n_cent,)),
            dma((span,)), dma((span,)), dma((span,)), dma((span,)),
            dma((devices,)), dma((devices,)),
        ],
        compiler_params=pltpu.CompilerParams(collective_id=0, has_side_effects=True),
        name="dedup",
    )(embeddings, assignment.reshape(1, rows), owner_map.reshape(clusters // LANES, LANES))
    centroid, representative, keep, top = pl.pallas_call(
        functools.partial(finish_kernel, per_owner, n_cent),
        out_shape=(
            shape((per_owner, width), F32),
            shape((per_owner, width), F32),
            shape((1, rows), F32),
            shape((1, 1), F32),
        ),
        in_specs=[vmem] * 4,
        out_specs=(vmem, vmem, vmem, pl.BlockSpec(memory_space=pltpu.SMEM)),
        scratch_shapes=[pltpu.VMEM((span * wide, LANES), F32)],
        name="finish",
    )(centroid, representative, back, meta)
    keep = keep.reshape(rows)

    def fast(embeddings, assignment, owner_map, centroid, representative, keep):
        return centroid, representative, keep

    def slow(embeddings, assignment, owner_map, centroid, representative, keep):
        return full_capacity(embeddings, assignment, owner_map)

    spilled = top[0, 0] >= SPILL
    return lax.cond(
        spilled, slow, fast, embeddings, assignment, owner_map, centroid, representative, keep
    )


def solution(mesh):
    in_specs = (P(("samp", "cent"), None), P(("samp", "cent")), P())
    out_specs = (P(("samp", "cent"), None), P(("samp", "cent"), None), P(("samp", "cent")))
    return jax.shard_map(
        on_device, mesh=mesh, in_specs=in_specs, out_specs=out_specs, check_vma=False
    )
```

```python
import functools

import jax
import jax.numpy as jnp
from jax import lax
from jax.experimental import pallas as pl
from jax.experimental.pallas import tpu as pltpu
from jax.sharding import PartitionSpec as P

EPSILON = 1e-06
SHARPNESS = 8.0
LANES = 128
HALF = LANES // 2
SPILL = 65536.0
BF = jnp.bfloat16
F32 = jnp.float32
I32 = jnp.int32
MESH = pl.DeviceIdType.MESH


def iota(shape, axis):
    return lax.broadcasted_iota(jnp.int32, shape, axis)


def row_dot(a, b):
    return lax.dot_general(a, b, (((1,), (1,)), ((), ())), preferred_element_type=F32)


def dot(a, b):
    return jnp.dot(a, b, preferred_element_type=F32)


def column_sum(a):
    return jnp.sum(a, axis=0, keepdims=True)


def flip(index, bits):
    step = 1
    while step <= bits:
        if bits & step:
            index = index + step * (1 - 2 * ((index // step) % 2))
        step *= 2
    return index


def plane_order(n_cent):
    return sorted(range(1, n_cent), key=lambda b: (b < n_cent // 2, b)) + [0]


def dedup_kernel(
    n_samp, n_cent, groups, per_owner, quota, bin_rows, lane_rows,
    emb_hbm, assign_hbm, owner_hbm, cent_ref, rep_ref, back_ref, meta_hbm,
    emb_ref, assign_ref, owner_ref, meta_ref, upper_ref, direct_ref, x_ref, tag_out_ref, tag_ref, bin_out_ref, bin_ref, note_out_ref, note_ref,
    lane_out_ref, mark_out_ref, mark_ref, col_ref, turn_ref, cent_out_ref, rep_out_ref, weight_ref,
    load_sem, own_sem, direct_out, direct_in, tag_out, tag_in, bin_out, bin_in, note_out, note_in,
    lane_out, lane_in, mark_out, mark_in, cent_send, cent_recv, rep_send, rep_recv, weight_out, weight_in,
):
    samp = lax.axis_index("samp")
    cent = lax.axis_index("cent")
    devices = n_samp * n_cent
    rows, width = emb_ref.shape
    table_rows = owner_ref.shape[0]
    span = devices // groups
    near = n_cent // groups
    each = per_owner // span
    wide = each * (width // LANES)
    slots = devices * quota
    late_slots = n_cent * HALF
    held = n_samp * HALF
    order = plane_order(n_cent)
    samps = [flip(samp, a) for a in range(n_samp)]
    cents = [flip(cent, b) for b in range(n_cent)]
    peers = [
        (i * n_samp + a, (samps[a], cents[b]))
        for i, b in enumerate(order)
        for a in range(n_samp)
        if a or b
    ]
    own = order.index(0) * n_samp

    def remote(source, target, sent, received, device):
        return pltpu.make_async_remote_copy(
            source, target, sent, received, device_id=device, device_id_type=MESH
        )

    parts = load_sem.shape[0] - 2
    part = rows // parts
    loads = [
        pltpu.make_async_copy(assign_hbm, assign_ref, load_sem.at[parts]),
        pltpu.make_async_copy(owner_hbm, owner_ref, load_sem.at[parts + 1]),
    ] + [
        pltpu.make_async_copy(
            emb_hbm.at[pl.ds(i * part, part)], emb_ref.at[pl.ds(i * part, part)], load_sem.at[i]
        )
        for i in range(parts)
    ]
    for copy in loads:
        copy.start()
    barrier = pltpu.get_barrier_semaphore()
    for _, device in peers:
        pl.semaphore_signal(barrier, inc=1, device_id=device, device_id_type=MESH)

    bin_ref[:, bin_rows:, :] = jnp.zeros((n_samp, HALF - bin_rows, width), BF)
    for b in range(1, n_cent):
        x_ref[slots + b * HALF + lane_rows:slots + (b + 1) * HALF, :] = jnp.zeros(
            (HALF - lane_rows, width), BF
        )
    upper_ref[...] = (iota(upper_ref.shape, 0) < iota(upper_ref.shape, 1)).astype(BF)

    for copy in loads:
        copy.wait()
    owner = owner_ref[...]
    owner_hot = (iota((table_rows, devices, LANES), 1) == owner[:, None, :]).astype(F32)
    before = dot(
        owner_hot.reshape(table_rows * devices, LANES).astype(BF), upper_ref[0:LANES, 0:LANES]
    ).reshape(table_rows, devices, LANES)
    base = jnp.zeros((devices, 1), F32)
    ranks = []
    for i in range(table_rows):
        ranks.append(column_sum(owner_hot[i] * (before[i] + base)))
        base = base + jnp.sum(owner_hot[i], axis=1, keepdims=True)
    table = jnp.concatenate([owner.astype(F32)] + ranks, axis=0).astype(BF)
    assign = assign_ref[...]
    found = dot(table, (iota((LANES, rows), 0) == assign % LANES).astype(BF))
    line = iota((table_rows, rows), 0) == assign // LANES
    owned = column_sum(jnp.where(line, found[0:table_rows, :], 0.0)).astype(I32)
    rank = column_sum(jnp.where(line, found[table_rows:, :], 0.0)).astype(I32)
    is_high = rank >= per_owner // 2
    fold = jnp.where(is_high, per_owner - 1 - rank, rank)
    place = fold % span
    own_cent = owned % n_cent
    to_samp = place // near
    to_cent = (own_cent // near) * near + place % near
    chosen = fold // span + jnp.where(is_high, each // 2, 0)
    apart = ((owned // n_cent) ^ to_samp) * near + (own_cent ^ to_cent)
    tag = (apart * each + chosen + 1).astype(F32)
    to_samp = to_samp ^ samp
    to_cent = to_cent ^ cent
    dest = to_samp
    for i, b in enumerate(order):
        dest = dest + jnp.where(to_cent == b, i * n_samp, 0)

    upper = upper_ref[0:rows, 0:rows]
    dest_hot = (iota((devices, rows), 0) == dest).astype(F32)
    within = column_sum(dest_hot * dot(dest_hot.astype(BF), upper)).astype(I32)
    is_late = within >= quota
    late_hot = ((iota((n_samp, rows), 0) == to_samp) & is_late).astype(F32)
    place = column_sum(late_hot * dot(late_hot.astype(BF), upper)).astype(I32)
    crowded = jnp.max(jnp.where(is_late & (place >= bin_rows), 1.0, 0.0), axis=1, keepdims=True)
    meta_ref[...] = jnp.where(
        iota((8, rows), 0) == 0, dest, jnp.where(is_late, HALF + place, within)
    )

    keep_meta = pltpu.make_async_copy(meta_ref, meta_hbm, own_sem.at[4])
    keep_meta.start()
    emb = emb_ref[...]
    unit = (emb * lax.rsqrt(jnp.sum(emb * emb, axis=1, keepdims=True) + EPSILON)).astype(BF)
    direct_seat = jnp.where(is_late, -1, dest * quota + within)
    block = 2 * LANES

    def pack_direct(start):
        hot = (iota((block, rows), 0) + start == direct_seat).astype(BF)
        direct_ref[start:start + block, :] = dot(hot, unit).astype(BF)

    def direct_copy(slot, device):
        at = pl.ds(slot * quota, quota)
        return remote(direct_ref.at[at], x_ref.at[at], direct_out, direct_in, device)

    def tag_copy(slot, device):
        return remote(tag_out_ref.at[slot], tag_ref.at[slot], tag_out, tag_in, device)

    def bin_copy(a):
        return remote(
            bin_out_ref.at[a], bin_ref.at[a, pl.ds(0, bin_rows)], bin_out, bin_in, (samps[a], cent)
        )

    def note_copy(a):
        return remote(note_out_ref.at[a], note_ref.at[a], note_out, note_in, (samps[a], cent))

    def lane_copy(b):
        return remote(
            lane_out_ref.at[b, pl.ds(0, lane_rows)], x_ref.at[pl.ds(slots + b * HALF, lane_rows)],
            lane_out, lane_in.at[b // 2], (samp, cents[b]),
        )

    def mark_copy(b):
        return remote(mark_out_ref.at[b], mark_ref.at[b], mark_out, mark_in, (samp, cents[b]))

    def cent_copy(slot, device):
        return remote(cent_out_ref.at[slot], cent_ref.at[slot], cent_send, cent_recv, device)

    def rep_copy(slot, device):
        return remote(rep_out_ref.at[slot], rep_ref.at[slot], rep_send, rep_recv, device)

    def weight_copy(slot, device):
        return remote(weight_ref.at[slot], back_ref.at[slot], weight_out, weight_in, device)

    def whole(ref, sent, received):
        return remote(ref, ref, sent, received, (samps[1], cent))

    all_direct = whole(direct_ref.at[pl.ds(0, slots - quota)], direct_out, direct_in)
    all_tags = whole(tag_ref.at[pl.ds(0, devices - 1)], tag_out, tag_in)
    all_bins = whole(bin_out_ref.at[pl.ds(0, n_samp - 1)], bin_out, bin_in)
    all_notes = whole(note_ref.at[pl.ds(0, n_samp - 1)], note_out, note_in)
    all_marks = whole(mark_ref.at[pl.ds(0, n_cent - 1)], mark_out, mark_in)
    all_cents = whole(cent_out_ref.at[pl.ds(0, span - 1)], cent_send, cent_recv)
    all_reps = whole(rep_out_ref.at[pl.ds(0, span - 1)], rep_send, rep_recv)
    all_weights = whole(weight_ref.at[pl.ds(0, devices - 1)], weight_out, weight_in)

    def some_lanes(b, count):
        return whole(lane_out_ref.at[pl.ds(0, count), pl.ds(0, lane_rows)], lane_out, lane_in.at[b // 2])

    owners = [
        (a * near + b, (samps[a], cents[b]))
        for b in sorted(range(near), key=lambda b: (b < near // 2, b))
        for a in range(n_samp)
        if a or b
    ]

    def send_direct(start):
        for slot, device in peers:
            if start <= slot * quota < start + block:
                direct_copy(slot, device).start()

    pack_direct(0)
    pl.semaphore_wait(barrier, devices - 1)
    send_direct(0)

    seat = jnp.where(is_late & (place < bin_rows), (to_samp % 2) * HALF + place, -1)
    notes = row_dot(
        jnp.concatenate([late_hot * tag, late_hot * to_cent.astype(F32)], axis=0).astype(BF),
        (iota((LANES, rows), 0) == seat).astype(BF),
    )
    note_out_ref[:, 0, :] = notes[0:n_samp, :] + LANES * notes[n_samp:, :]
    seat = jnp.where(is_late & (place < bin_rows), to_samp * bin_rows + place, -1)
    hot = (iota((n_samp * bin_rows, rows), 0) == seat).astype(BF)
    bin_out_ref[...] = dot(hot, unit).astype(BF).reshape(n_samp, bin_rows, width)
    for a in range(1, n_samp):
        note_copy(a).start()
    for a in range(1, n_samp):
        bin_copy(a).start()
    for start in range(block, slots, block):
        pack_direct(start)
        send_direct(start)
    pack = LANES // quota
    seat = jnp.where(is_late, -1, (dest % pack) * quota + within)
    tag_out_ref[:, 0, :] = row_dot(
        (dest_hot * tag).astype(BF), (iota((LANES, rows), 0) == seat).astype(BF)
    )
    for slot, device in peers:
        tag_copy(slot, device).start()
    mine = pl.ds(own * quota, quota)
    local = [
        pltpu.make_async_copy(bin_out_ref.at[0], bin_ref.at[0, pl.ds(0, bin_rows)], own_sem.at[0]),
        pltpu.make_async_copy(note_out_ref.at[0], note_ref.at[0], own_sem.at[1]),
        pltpu.make_async_copy(direct_ref.at[mine], x_ref.at[mine], own_sem.at[2]),
        pltpu.make_async_copy(tag_out_ref.at[own], tag_ref.at[own], own_sem.at[3]),
    ]
    for copy in local:
        copy.start()
    for copy in local:
        copy.wait()

    all_notes.wait_recv()
    code = jnp.concatenate(
        [note_ref[j] + note_ref[j + 1] for j in range(0, n_samp, 2)], axis=1
    ).astype(I32)
    tag = code % LANES
    to_cent = code // LANES
    lane_hot = ((iota((n_cent, held), 0) == to_cent) & (tag > 0)).astype(F32)
    place = column_sum(lane_hot * dot(lane_hot.astype(BF), upper_ref[0:held, 0:held])).astype(I32)
    fits = place < jnp.where(to_cent == 0, HALF, lane_rows)
    crowded = jnp.maximum(
        crowded, jnp.max(jnp.where((tag > 0) & jnp.logical_not(fits), 1.0, 0.0), axis=1, keepdims=True)
    )
    fits = fits & (tag > 0)
    which = iota((16, held), 0)
    at = iota((16, held), 1)
    pieces = jnp.where(
        which == 0, tag, jnp.where(which == 1, at % HALF, jnp.where(which == 2, at // HALF, 0))
    ).astype(F32).astype(BF)
    for b in range(n_cent):
        seat = jnp.where(fits & (to_cent == b), (b % 2) * HALF + place, -1)
        marks = row_dot(pieces, (iota((LANES, held), 0) == seat).astype(BF))
        mark_out_ref[b] = marks[0:1, :] + LANES * (marks[1:2, :] + HALF * marks[2:3, :])
    hot = (iota((late_slots, held), 0) == jnp.where(fits, to_cent * HALF + place, -1)).astype(BF)
    all_bins.wait_recv()
    lane_out_ref[...] = (
        dot(hot, bin_ref[...].reshape(held, width)).astype(BF).reshape(n_cent, HALF, width)
    )
    for b in order[:-1]:
        mark_copy(b).start()
    for b in order[:-1]:
        lane_copy(b).start()
    local = [
        pltpu.make_async_copy(lane_out_ref.at[0], x_ref.at[pl.ds(slots, HALF)], own_sem.at[0]),
        pltpu.make_async_copy(mark_out_ref.at[0], mark_ref.at[0], own_sem.at[1]),
    ]
    for copy in local:
        copy.start()
    for copy in local:
        copy.wait()

    def columns(tags, at):
        for start in range(0, tags.shape[1], LANES):
            chunk = jnp.broadcast_to(tags[:, start:start + LANES], (LANES, LANES))
            col_ref[at + start:at + start + LANES, :] = jnp.transpose(chunk)

    def score(low, high, fresh, tags):
        alike = jnp.zeros(tags.shape, F32)
        close = jnp.zeros(tags.shape, F32)
        for start in range(low, high, block):
            end = min(start + block, high)
            gram = row_dot(x_ref[start:end, :], fresh)
            left = col_ref[start:end, :]
            same = jnp.concatenate([left] * (tags.shape[1] // LANES), axis=1) == tags
            alike = alike + column_sum(jnp.where(same, gram, 0.0))
            close = close + column_sum(jnp.where(same, jnp.exp(SHARPNESS * (gram - 1.0)), 0.0))
        return alike, close

    def hit(tags):
        return (iota((per_owner, tags.shape[1]), 0) + 1).astype(F32) == tags

    all_tags.wait_recv()
    tags = []
    for start in range(0, devices, pack):
        total = tag_ref[start]
        for j in range(start + 1, start + pack):
            total = total + tag_ref[j]
        tags.append(total)
    tags = jnp.concatenate(tags, axis=1)
    columns(tags, 0)
    all_direct.wait_recv()
    x = x_ref[0:slots, :]
    similar, density = score(0, slots, x, tags)
    sums = dot(hit(tags).astype(BF), x)

    all_marks.wait_recv()
    sources = []
    columns_of = []
    for b in range(0, n_cent, 2):
        code = (mark_ref[b] + mark_ref[b + 1]).astype(I32)
        fresh_tags = (code % LANES).astype(F32)
        columns_of.append(HALF + (code // LANES) % HALF)
        lane = iota((1, LANES), 1)
        sources.append(
            code // (LANES * HALF)
            + n_samp * jnp.where(lane < HALF, order.index(b), order.index(b + 1))
        )
        at = slots + b * HALF
        columns(fresh_tags, at)
        some_lanes(b, 2 if b else 1).wait_recv()
        fresh = x_ref[at:at + LANES, :]
        sums = sums + dot(hit(fresh_tags).astype(BF), fresh)
        if b == n_cent - 2:
            inverse = lax.rsqrt(jnp.sum(sums * sums, axis=1, keepdims=True) + EPSILON)
        alike, close = score(0, at + LANES, fresh, fresh_tags)
        more_alike, more_close = score(at, at + LANES, x_ref[0:at, :], tags)
        similar = jnp.concatenate([similar + more_alike, alike], axis=1)
        density = jnp.concatenate([density + more_close, close], axis=1)
        tags = jnp.concatenate([tags, fresh_tags], axis=1)

    def fold_out(value, target):
        for i in range(width // LANES):
            turn_ref[pl.ds(i, per_owner, stride=width // LANES), :] = value[:, i * LANES:(i + 1) * LANES]
        target[...] = turn_ref[...].astype(BF).reshape(span, wide, LANES)

    fold_out(sums * inverse, cent_out_ref)
    for slot, device in owners:
        cent_copy(slot, device).start()
    hits = hit(tags)
    valid = tags > 0.0
    scale = column_sum(jnp.where(hits, inverse, 0.0))
    weight = jnp.where(
        valid, jnp.exp(1.0 - similar * scale) / jnp.where(valid, density, 1.0), 0.0
    )
    mixed = dot(jnp.where(hits, weight, 0.0).astype(BF), x_ref[...])
    fold_out(
        mixed * lax.rsqrt(jnp.sum(mixed * mixed, axis=1, keepdims=True) + EPSILON), rep_out_ref
    )
    for slot, device in owners:
        rep_copy(slot, device).start()

    lane = iota((1, slots), 1)
    sources = jnp.concatenate([lane // quota] + sources, axis=1)
    columns_of = jnp.concatenate([lane % quota] + columns_of, axis=1)
    spread = jnp.where(iota((devices, slots + late_slots), 0) == sources, weight, 0.0)
    high = spread.astype(BF)
    spread = row_dot(
        jnp.concatenate([high, (spread - high.astype(F32)).astype(BF)], axis=0),
        (iota((LANES, slots + late_slots), 0) == columns_of).astype(BF),
    )
    flag = jnp.where((iota((1, LANES), 1) == LANES - 1) & (crowded > 0.0), SPILL, 0.0)
    weight_ref[:, 0, :] = spread[0:devices, :] + spread[devices:, :] + flag
    for slot, device in peers:
        weight_copy(slot, device).start()
    local = [
        pltpu.make_async_copy(cent_out_ref.at[0], cent_ref.at[0], own_sem.at[0]),
        pltpu.make_async_copy(rep_out_ref.at[0], rep_ref.at[0], own_sem.at[1]),
        pltpu.make_async_copy(weight_ref.at[own], back_ref.at[own], own_sem.at[2]),
    ]
    for copy in local:
        copy.start()

    some_lanes(0, n_cent - 1).wait_send()
    for copies in (all_notes, all_bins, all_marks, all_direct, all_tags):
        copies.wait_send()
    keep_meta.wait()
    for copy in local:
        copy.wait()
    for copies in (all_cents, all_reps, all_weights):
        copies.wait()


def finish_kernel(
    per_owner, n_cent, cent_ref, rep_ref, back_ref, meta_ref, centroid_ref, representative_ref, keep_ref, top_ref, turn_ref
):
    span, wide, _ = cent_ref.shape
    each = per_owner // span
    chunks = wide // each
    devices = back_ref.shape[0]
    rows = meta_ref.shape[1]
    near = n_cent * span // devices
    mine = lax.axis_index("samp") * near + lax.axis_index("cent") % near
    back = back_ref[:, 0, :]
    top_ref[0, 0] = jnp.max(back)
    rank = iota((per_owner, per_owner), 0)
    is_high = rank >= per_owner // 2
    fold = jnp.where(is_high, per_owner - 1 - rank, rank)
    source = ((fold % span) ^ mine) * each + fold // span + jnp.where(is_high, each // 2, 0)
    order = (iota((per_owner, per_owner), 1) == source).astype(BF)
    for got, out in ((cent_ref, centroid_ref), (rep_ref, representative_ref)):
        turn_ref[...] = got[...].reshape(span * wide, LANES).astype(F32)
        flat = jnp.concatenate(
            [turn_ref[pl.ds(i, per_owner, stride=chunks), :] for i in range(chunks)], axis=1
        )
        out[...] = dot(order, flat.astype(BF))
    meta = meta_ref[...]
    dest_hot = (iota((devices, rows), 0) == meta[0:1, :]).astype(F32)
    spread = lax.dot_general(
        back, dest_hot, (((0,), (0,)), ((), ())),
        preferred_element_type=F32, precision=lax.Precision.HIGHEST,
    )
    hit = iota((LANES, rows), 0) == meta[1:2, :]
    keep_ref[...] = column_sum(jnp.where(hit, spread, 0.0))


def all_pairs(arrived, arrived_tags, validity, block_size):
    slot_count, feature_width = arrived.shape
    block_count = slot_count // block_size

    def score_block(pieces):
        block_rows, block_tags = pieces
        gram = jnp.einsum("rd,qd->rq", block_rows, arrived, preferred_element_type=jnp.float32)
        same_cluster = (block_tags[:, None] == arrived_tags[None, :]) & validity[None, :]
        similar = jnp.sum(jnp.where(same_cluster, gram, 0.0), axis=1)
        density = jnp.sum(jnp.where(same_cluster, jnp.exp(SHARPNESS * (gram - 1.0)), 0.0), axis=1)
        return (similar, density)

    similar, density = lax.map(
        score_block,
        (
            arrived.reshape(block_count, block_size, feature_width),
            arrived_tags.reshape(block_count, block_size),
        ),
    )
    return (similar.reshape(slot_count), density.reshape(slot_count))


def full_capacity(embeddings, assignment, owner_map):
    row_count, feature_width = embeddings.shape
    devices = lax.axis_size("samp") * lax.axis_size("cent")
    clusters = owner_map.shape[0]
    per_owner = clusters // devices
    capacity = 4 * row_count // devices
    slot_count = devices * capacity
    unit_rows = (
        embeddings * lax.rsqrt(jnp.sum(embeddings * embeddings, axis=1, keepdims=True) + EPSILON)
    ).astype(jnp.bfloat16)
    destination = owner_map[assignment]
    cluster_order = jnp.argsort(owner_map, stable=True)
    position = (
        jnp.zeros((clusters,), jnp.int32)
        .at[cluster_order]
        .set(jnp.arange(clusters, dtype=jnp.int32))
    )
    local_rank = position[assignment] - destination * per_owner
    dest_onehot = (destination[:, None] == jnp.arange(devices, dtype=jnp.int32)[None, :]).astype(
        jnp.int32
    )
    within_rank = jnp.sum(jnp.cumsum(dest_onehot, axis=0) * dest_onehot, axis=1) - 1
    slot_index = destination * capacity + within_rank
    outgoing = jnp.zeros((slot_count, feature_width), jnp.bfloat16).at[slot_index].set(unit_rows)
    labels = (
        jnp.zeros((slot_count,), jnp.bfloat16)
        .at[slot_index]
        .set((local_rank + 1).astype(jnp.bfloat16))
    )
    arrived, arrived_labels = (
        lax.all_to_all(outgoing, ("samp", "cent"), split_axis=0, concat_axis=0, tiled=True),
        lax.all_to_all(labels, ("samp", "cent"), split_axis=0, concat_axis=0, tiled=True),
    )
    arrived_tags = arrived_labels.astype(jnp.int32) - 1
    validity = arrived_tags >= 0
    block_size = min(512, slot_count)
    similar, density = all_pairs(arrived, arrived_tags, validity, block_size)
    member = arrived_tags[None, :] == jnp.arange(per_owner, dtype=jnp.int32)[:, None]
    member_bf = member.astype(jnp.bfloat16)
    cluster_sums = jnp.dot(member_bf, arrived, preferred_element_type=jnp.float32)
    inverse_norm = lax.rsqrt(jnp.sum(cluster_sums * cluster_sums, axis=1) + EPSILON)
    row_scale = jnp.sum(member.astype(jnp.float32) * inverse_norm[:, None], axis=0)
    spread = 1.0 - similar * row_scale
    weight = jnp.where(validity, jnp.exp(spread) / jnp.where(validity, density, 1.0), 0.0)
    weighted = jnp.dot(
        member_bf * weight.astype(jnp.bfloat16)[None, :],
        arrived,
        preferred_element_type=jnp.float32,
    )
    centroid = cluster_sums * inverse_norm[:, None]
    representative = weighted * lax.rsqrt(
        jnp.sum(weighted * weighted, axis=1, keepdims=True) + EPSILON
    )
    returned = lax.all_to_all(weight, ("samp", "cent"), split_axis=0, concat_axis=0, tiled=True)
    keep_weight = returned[slot_index]
    return (centroid, representative, keep_weight)


def on_device(embeddings, assignment, owner_map):
    rows, width = embeddings.shape
    n_samp = lax.axis_size("samp")
    n_cent = lax.axis_size("cent")
    devices = n_samp * n_cent
    clusters = owner_map.shape[0]
    per_owner = clusters // devices
    groups = max(1, 2 * devices // per_owner)
    quota = -(-rows // devices // 16) * 16
    bin_rows = 48
    lane_rows = 56
    span = devices // groups
    wide = per_owner // span * (width // LANES)
    slots = devices * quota
    late_slots = n_cent * HALF
    depth = max(rows, n_samp * HALF)
    vmem = pl.BlockSpec(memory_space=pltpu.VMEM)
    anywhere = pl.BlockSpec(memory_space=pl.ANY)
    shape = jax.ShapeDtypeStruct
    dma = pltpu.SemaphoreType.DMA
    centroid, representative, back, meta = pl.pallas_call(
        functools.partial(
            dedup_kernel, n_samp, n_cent, groups, per_owner, quota, bin_rows, lane_rows
        ),
        out_shape=(
            shape((span, wide, LANES), BF),
            shape((span, wide, LANES), BF),
            shape((devices, 1, LANES), F32),
            shape((8, rows), I32),
        ),
        in_specs=[anywhere] * 3,
        out_specs=(anywhere,) * 4,
        scratch_shapes=[
            pltpu.VMEM((rows, width), F32),
            pltpu.VMEM((1, rows), I32),
            pltpu.VMEM((clusters // LANES, LANES), I32),
            pltpu.VMEM((8, rows), I32),
            pltpu.VMEM((depth, depth), BF),
            pltpu.VMEM((slots, width), BF),
            pltpu.VMEM((slots + late_slots, width), BF),
            pltpu.VMEM((devices, 1, LANES), F32),
            pltpu.VMEM((devices, 1, LANES), F32),
            pltpu.VMEM((n_samp, bin_rows, width), BF),
            pltpu.VMEM((n_samp, HALF, width), BF),
            pltpu.VMEM((n_samp, 1, LANES), F32),
            pltpu.VMEM((n_samp, 1, LANES), F32),
            pltpu.VMEM((n_cent, HALF, width), BF),
            pltpu.VMEM((n_cent, 1, LANES), F32),
            pltpu.VMEM((n_cent, 1, LANES), F32),
            pltpu.VMEM((slots + late_slots, LANES), F32),
            pltpu.VMEM((span * wide, LANES), F32),
            pltpu.VMEM((span, wide, LANES), BF),
            pltpu.VMEM((span, wide, LANES), BF),
            pltpu.VMEM((devices, 1, LANES), F32),
            dma((6,)), dma((5,)),
            dma, dma, dma, dma, dma, dma, dma, dma,
            dma, dma((n_cent // 2,)), dma, dma, dma, dma, dma, dma, dma, dma,
        ],
        compiler_params=pltpu.CompilerParams(collective_id=0, has_side_effects=True),
        name="dedup",
    )(embeddings, assignment.reshape(1, rows), owner_map.reshape(clusters // LANES, LANES))
    centroid, representative, keep, top = pl.pallas_call(
        functools.partial(finish_kernel, per_owner, n_cent),
        out_shape=(
            shape((per_owner, width), F32),
            shape((per_owner, width), F32),
            shape((1, rows), F32),
            shape((1, 1), F32),
        ),
        in_specs=[vmem] * 4,
        out_specs=(vmem, vmem, vmem, pl.BlockSpec(memory_space=pltpu.SMEM)),
        scratch_shapes=[pltpu.VMEM((span * wide, LANES), F32)],
        name="finish",
    )(centroid, representative, back, meta)
    keep = keep.reshape(rows)

    def fast(embeddings, assignment, owner_map, centroid, representative, keep):
        return centroid, representative, keep

    def slow(embeddings, assignment, owner_map, centroid, representative, keep):
        return full_capacity(embeddings, assignment, owner_map)

    spilled = top[0, 0] >= SPILL
    return lax.cond(
        spilled, slow, fast, embeddings, assignment, owner_map, centroid, representative, keep
    )


def solution(mesh):
    in_specs = (P(("samp", "cent"), None), P(("samp", "cent")), P())
    out_specs = (P(("samp", "cent"), None), P(("samp", "cent"), None), P(("samp", "cent")))
    return jax.shard_map(
        on_device, mesh=mesh, in_specs=in_specs, out_specs=out_specs, check_vma=False
    )
```
